1024 devices in a mesh: row: 64 (over y, x_lo, core), col: 16 (over z, x_hi).
Axes of the slice: x: 8 (x_hi: 2, x_lo: 4; x = x_hi * 4 + x_lo), y: 8, z: 8, core: 2. Of those that a mesh axis runs over, the one named last changes fastest.
Arguments:
- field: bfloat16 [64, 1536, 2, 2, 512], P(None, 'row', None, None, 'col'), may hold values from -6 to 6
- coef: float32 [1536, 512], P('row', 'col'), may hold values from 0.3 to 3
- table: bfloat16 [64, 1024, 1536], P('row'), may hold values from -0.15625 to 0.15625
- order_ids: int32 [64], P('row'), may hold values from 0 to 1023, as said below
- inverses: bfloat16 [1024, 512, 512], P(('row', 'col')), may hold values from -0.25 to 0.25
- degree_owner: int32 [1024], replicated, may hold values from 0 to 1023, each once
Outputs:
- synthesized: bfloat16 [64, 1536, 2, 2, 512], P(None, 'row', None, None, 'col')
The draws below stay inside these ranges and needn't reach their ends.
Inputs may be any that keep to these rules, and one draw needn't show every extreme that they name: `order_ids`: distinct orders; 0 and 1023 are always among them. `degree_owner`: every degree appears exactly once.
All inputs are finite; a program needn't handle non-finite values.
Results may differ from the reference program's by a relative error of at most 0.0064.
Values may be sent and summed in bfloat16 or wider, within the bound.
A program may use at most 32 MiB of HBM per device.

```python
import math
import jax
import jax.numpy as jnp
from jax import lax

LDEG = 1024
LAT = 1536
RADII = 512
FIELDS = 2
ORDERS = 64


def draw_order_ids(key, part):
    first_key = jax.random.fold_in(key, 11)
    second_key = jax.random.fold_in(key, 23)
    middle = 1 + jax.random.permutation(first_key, LDEG - 2)[:ORDERS - 2]
    values = jnp.concatenate([jnp.array([0, LDEG - 1], jnp.int32), middle.astype(jnp.int32)])
    return values[jax.random.permutation(second_key, ORDERS)].astype(jnp.int32)


def block_levels(key, extent, split, low, top_value):
    level, own = 1.0, jax.random.fold_in(key, 6)
    for dim, blocks in split:
        draws = jnp.exp(jax.random.uniform(jax.random.fold_in(own, dim), (blocks,), jnp.float32, low / len(split), top_value / len(split)))
        level = level * jnp.repeat(draws, extent[dim] // blocks).reshape([-1 if axis == dim else 1 for axis in range(len(extent))])
    return level


def scatter_about(key, dims, width, most, pieces=(), kind=jnp.bfloat16):
    gain = block_levels(key, dims, pieces, -0.22, 0.18) if pieces else 1.0
    drawn = jax.random.normal(key, dims, jnp.float32) * width * gain
    return jnp.minimum(jnp.maximum(drawn, -most), most).astype(kind)


def setup_inputs(seed: int = 0) -> dict:
    streams_of = jax.random.split(jax.random.key(seed), 7)
    return {
        "field": scatter_about(streams_of[0], (ORDERS, LAT, FIELDS, 2, RADII), 1.0, 6.0, ((1, 64), (4, 16))),
        "coef": jnp.clip(jnp.exp(math.log(3.0) - 2.3025851 * jax.random.uniform(streams_of[1], (LAT, RADII), jnp.float32) ** block_levels(streams_of[1], (LAT, RADII), ((0, 64), (1, 16)), -0.2, 0.2)), 0.3, 3.0),
        "table": scatter_about(streams_of[2], (ORDERS, LDEG, LAT), LAT ** -0.5, 0.15625, ((0, 64),)),
        "order_ids": draw_order_ids(jax.random.fold_in(streams_of[6], 71), 0),
        "inverses": scatter_about(streams_of[4], (LDEG, RADII, RADII), RADII ** -0.5, 0.25, ((0, 1024),)),
        "degree_owner": jax.random.permutation(streams_of[5], LDEG).astype(jnp.int32),
    }


def reference(field, coef, table, order_ids, inverses, degree_owner):
    weighted = (field.astype(jnp.float32) * coef[None, :, None, None, :]).astype(jnp.bfloat16)
    degrees = lax.iota(jnp.int32, LDEG)

    def analyze(inputs):
        table_rows, columns, order_id = inputs
        product = jnp.dot(table_rows, columns.reshape(LAT, FIELDS * 2 * RADII), preferred_element_type=jnp.float32)
        product = jnp.where((degrees >= order_id)[:, None], product, 0.0)
        return product.astype(jnp.bfloat16).reshape(LDEG, FIELDS, 2, RADII)

    spectral = lax.map(analyze, (table, weighted, order_ids))
    placed = jnp.take(spectral, degree_owner, axis=1)
    solved_placed = jnp.einsum("kpfcs,prs->kpfcr", placed.astype(jnp.float32), inverses.astype(jnp.float32)).astype(jnp.bfloat16)
    inverse_order = jnp.zeros((LDEG,), jnp.int32).at[degree_owner].set(degrees)
    solved = jnp.take(solved_placed, inverse_order, axis=1)

    def synthesize(inputs):
        table_rows, coeffs = inputs
        product = jnp.dot(table_rows.T, coeffs.reshape(LDEG, FIELDS * 2 * RADII), preferred_element_type=jnp.float32)
        return product.astype(jnp.bfloat16).reshape(LAT, FIELDS, 2, RADII)

    return lax.map(synthesize, (table, solved))
```

```python
import functools

import jax
import jax.numpy as jnp
from jax import lax
from jax.experimental import pallas as pl
from jax.experimental.pallas import tpu as pltpu
from jax.sharding import PartitionSpec as P

MESH = pl.DeviceIdType.MESH
BF = jnp.bfloat16
F32 = jnp.float32


class Plan:
    def __init__(self, rows, cols, lat, radii, members):
        self.rows, self.cols = rows, cols
        self.co = 2
        self.xl = 4 if rows % 32 == 0 else 2
        self.y = rows // (self.xl * self.co)
        self.na = self.y * self.co
        self.nb = cols * self.xl
        self.deg = rows * cols
        self.t = lat // rows
        self.rd = radii // cols
        self.fc = members
        self.j = members * self.rd


def kernel(pn, field, coef, table, inv, deg, order, out,
           fv, cv, tv, iv, dv, s1, r1, sf, perm, tp, tt, w, sp, e1, e2, d2, o2,
           g1, g2, h1, ob, vb, zv, insem, ssem, rsem):
    rows, cols, na, nb, nt, nj = pn.rows, pn.cols, pn.na, pn.nb, pn.t, pn.j
    me_row, me_col = lax.axis_index("row"), lax.axis_index("col")
    co = me_row % pn.co
    xl = (me_row // pn.co) % pn.xl
    y = me_row // (pn.co * pn.xl)
    me_a = y * pn.co + co
    me_b = me_col * pn.xl + xl

    def row_peer(s):
        j = (me_row + s) % rows
        return j, (j, me_col)

    def a_peer(s):
        a = (me_a + s) % na
        return a, (((a // pn.co) * pn.xl + xl) * pn.co + a % pn.co, me_col)

    def b_peer(s):
        b = (me_b + s) % nb
        return b, ((y * pn.xl + b % pn.xl) * pn.co + co, b // pn.xl)

    loads = [(field, fv), (coef, cv), (deg, dv), (table, tv), (inv, iv)]
    loads = [pltpu.make_async_copy(src, dst, insem.at[i]) for i, (src, dst) in enumerate(loads)]
    for c in loads:
        c.start()

    barrier = pltpu.get_barrier_semaphore()

    def greet(peer, s, _):
        pl.semaphore_signal(barrier, inc=1, device_id=peer(s)[1], device_id_type=MESH)
        return 0

    lax.fori_loop(1, rows, functools.partial(greet, row_peer), 0)
    lax.fori_loop(1, nb, functools.partial(greet, b_peer), 0)

    loads[0].wait()
    loads[1].wait()
    eye = (lax.broadcasted_iota(jnp.int32, (rows, rows), 0)
           == lax.broadcasted_iota(jnp.int32, (rows, rows), 1)).astype(F32).astype(BF)
    tc = 4
    for i in range(nt // tc):
        x = fv[pl.ds(i * tc, tc)].reshape(tc * nj, rows)
        yv = lax.dot_general(eye, x, (((1,), (1,)), ((), ())), preferred_element_type=F32)
        for t in range(tc):
            sf[pl.ds((i * tc + t) * rows, rows), :] = yv[:, t * nj:(t + 1) * nj]
    c4 = jnp.concatenate([cv[...]] * pn.fc, axis=1)
    for k in range(0, rows, 2):
        w0 = sf[pl.ds(k, nt, stride=rows), :] * c4
        w1 = sf[pl.ds(k + 1, nt, stride=rows), :] * c4
        s1[pl.ds(k * (nt // 8), nt // 4)] = jnp.concatenate([w0, w1], axis=0).astype(BF).reshape(nt // 4, 8, nj)

    pl.semaphore_wait(barrier, rows - 1 + nb - 1)

    def exchange(stage, n, peer, src_of, dst, me):
        def send(s, _):
            i, dev = peer(s)
            pltpu.make_async_remote_copy(
                src_ref=src_of(i), dst_ref=dst, send_sem=ssem.at[stage], recv_sem=rsem.at[stage],
                device_id=dev, device_id_type=MESH).start()
            return 0
        lax.fori_loop(1, n, send, 0)
        pltpu.make_async_copy(src_of(me), dst, rsem.at[stage]).start()

    def arrived(stage, buf):
        pltpu.make_async_copy(buf, buf, rsem.at[stage]).wait()

    def sent(stage, part):
        pltpu.make_async_copy(part, part, ssem.at[stage]).wait()

    u = nt // 8
    exchange(0, rows, row_peer, lambda i: s1.at[pl.ds(i * u, u)], r1.at[pl.ds(me_row * u, u)], me_row)

    loads[2].wait()
    n_deg = pn.deg
    owner = jnp.broadcast_to(dv[...], (128, n_deg)).T
    lanes = min(128, n_deg)
    owner = owner[:, :lanes]
    for c in range(n_deg // lanes):
        lane = lax.broadcasted_iota(jnp.int32, (n_deg, lanes), 1) + c * lanes
        hit = jnp.logical_and(owner == lane, lane >= order[0])
        perm[:, c * lanes:(c + 1) * lanes] = jnp.where(hit, 1.0, 0.0).astype(F32).astype(BF)
    loads[3].wait()
    qb = min(128, n_deg)

    def permute(i, _):
        q = pl.multiple_of(i * qb, qb)
        block = jnp.dot(perm[pl.ds(q, qb), :], tv[0], preferred_element_type=F32).astype(BF)
        tp[pl.ds(q, qb), :] = block
        tt[:, pl.ds(q, qb)] = block.T
        return 0

    lax.fori_loop(0, n_deg // qb, permute, 0)

    arrived(0, r1)
    sg = max(1, na // 4)
    columns = r1[...].reshape(rows * nt, nj)
    for i in range(na // sg):
        block = jnp.dot(tp[pl.ds(i * sg * nb, sg * nb), :], columns, preferred_element_type=F32)
        sp[pl.ds(i * sg, sg)] = block.astype(BF).reshape(sg, nb, nj)
    exchange(1, na, a_peer, lambda i: sp.at[i], e1.at[me_a], me_a)

    loads[4].wait()
    cg = min(4, cols)
    nr, nn = cg * pn.rd, cg * nj
    n_id = lax.broadcasted_iota(jnp.int32, (nr, nn), 1)
    r_id = lax.broadcasted_iota(jnp.int32, (nr, nn), 0)
    spread = jnp.where(r_id == (n_id // nj) * pn.rd + n_id % pn.rd, 1.0, 0.0).astype(F32).astype(BF)
    fc_id = (lax.broadcasted_iota(jnp.int32, (1, nn), 1) % nj) // pn.rd

    def widen(g, _):
        part = iv[0, pl.ds(pl.multiple_of(g * nr, nr), nr), :]
        x = lax.dot_general(part, spread, (((0,), (0,)), ((), ())), preferred_element_type=F32)
        for f in range(pn.fc):
            z = jnp.where(fc_id == f, x, 0.0).astype(BF)
            w[:, f, :, pl.ds(pl.multiple_of(g * nn, nn), nn)] = z.reshape(cols, pn.rd, nn)
        return 0

    lax.fori_loop(0, cols // cg, widen, 0)

    arrived(1, e1)
    sf[pl.ds(0, na * nb), :] = e1[...].reshape(na * nb, nj).astype(F32)
    for b in range(nb):
        e2[b] = sf[pl.ds(b, na, stride=nb), :].astype(BF)
    corner = d2.at[pl.ds(pl.multiple_of(xl * na, na), na), pl.ds(pl.multiple_of(me_col * nj, nj), nj)]
    exchange(2, nb, b_peer, lambda i: e2.at[i], corner, me_b)

    arrived(2, d2)
    for g in range(cols // cg):
        right = w[:, :, :, g * nn:(g + 1) * nn].reshape(cols * nj, nn)
        o2[:, g * nn:(g + 1) * nn] = jnp.dot(d2[...], right, preferred_element_type=F32).astype(BF)

    def tile_of(b):
        return o2.at[pl.ds(pl.multiple_of((b % pn.xl) * na, na), na),
                     pl.ds(pl.multiple_of((b // pn.xl) * nj, nj), nj)]

    exchange(3, nb, b_peer, tile_of, g1.at[me_b], me_b)
    arrived(3, g1)
    sf[pl.ds(0, na * nb), :] = g1[...].reshape(na * nb, nj).astype(F32)
    for a in range(na):
        g2[a] = sf[pl.ds(a, nb, stride=na), :].astype(BF)
    exchange(4, na, a_peer, lambda i: g2.at[i], h1.at[me_a], me_a)

    arrived(4, h1)
    coeffs = h1[...].reshape(n_deg, nj)
    lg = rows * nt // 4
    for i in range(4):
        block = jnp.dot(tt[pl.ds(i * lg, lg), :], coeffs, preferred_element_type=F32)
        ob[pl.ds(i * lg // 8, lg // 8)] = block.astype(BF).reshape(lg // 8, 8, nj)
    exchange(5, rows, row_peer, lambda i: ob.at[pl.ds(i * u, u)], vb.at[pl.ds(me_row * u, u)], me_row)

    arrived(5, vb)
    sf[...] = vb[...].reshape(rows * nt, nj).astype(F32)
    eye_j = (lax.broadcasted_iota(jnp.int32, (nj, nj), 0)
             == lax.broadcasted_iota(jnp.int32, (nj, nj), 1)).astype(F32).astype(BF)
    for t in range(nt):
        z = sf[pl.ds(t, rows, stride=nt), :].astype(BF)
        zv[t] = lax.dot_general(eye_j, z, (((1,), (1,)), ((), ())), preferred_element_type=F32).astype(BF)
    done = pltpu.make_async_copy(zv, out, insem.at[0])
    done.start()
    sent(0, s1.at[pl.ds(0, (rows - 1) * u)])
    sent(1, sp.at[pl.ds(0, na - 1)])
    sent(2, e2.at[pl.ds(0, nb - 1)])
    sent(3, g1.at[pl.ds(0, nb - 1)])
    sent(4, g2.at[pl.ds(0, na - 1)])
    sent(5, ob.at[pl.ds(0, (rows - 1) * u)])
    done.wait()


def solution(mesh):
    rows, cols = mesh.shape["row"], mesh.shape["col"]

    def per_device(field, coef, table, order_ids, inverses, degree_owner):
        orders, nt, f, c, rd = field.shape
        pn = Plan(rows, cols, table.shape[2], rd * cols, f * c)
        na, nb, nj, n_deg = pn.na, pn.nb, pn.j, pn.deg
        lat = rows * nt
        field = jnp.transpose(field, (1, 2, 3, 4, 0)).reshape(nt, nj, orders)
        deg = degree_owner.reshape(pn.y, pn.xl, pn.co, cols)
        deg = jnp.transpose(deg, (0, 2, 3, 1)).reshape(1, n_deg)
        anyspace = pl.BlockSpec(memory_space=pl.ANY)
        out = pl.pallas_call(
            functools.partial(kernel, pn),
            out_shape=jax.ShapeDtypeStruct((nt, nj, orders), BF),
            in_specs=[anyspace] * 5 + [pl.BlockSpec(memory_space=pltpu.SMEM)],
            out_specs=anyspace,
            scratch_shapes=[
                pltpu.VMEM((nt, nj, orders), BF),
                pltpu.VMEM((nt, rd), F32),
                pltpu.VMEM((1, n_deg, lat), BF),
                pltpu.VMEM((1, cols * rd, cols * rd), BF),
                pltpu.VMEM((1, n_deg), jnp.int32),
                pltpu.VMEM((lat // 8, 8, nj), BF),
                pltpu.VMEM((lat // 8, 8, nj), BF),
                pltpu.VMEM((lat, nj), F32),
                pltpu.VMEM((n_deg, n_deg), BF),
                pltpu.VMEM((n_deg, lat), BF),
                pltpu.VMEM((lat, n_deg), BF),
                pltpu.VMEM((cols, pn.fc, rd, cols * nj), BF),
                pltpu.VMEM((na, nb, nj), BF),
                pltpu.VMEM((na, nb, nj), BF),
                pltpu.VMEM((nb, na, nj), BF),
                pltpu.VMEM((rows, cols * nj), BF),
                pltpu.VMEM((rows, cols * nj), BF),
                pltpu.VMEM((nb, na, nj), BF),
                pltpu.VMEM((na, nb, nj), BF),
                pltpu.VMEM((na, nb, nj), BF),
                pltpu.VMEM((lat // 8, 8, nj), BF),
                pltpu.VMEM((lat // 8, 8, nj), BF),
                pltpu.VMEM((nt, nj, orders), BF),
                pltpu.SemaphoreType.DMA((5,)),
                pltpu.SemaphoreType.DMA((6,)),
                pltpu.SemaphoreType.DMA((6,)),
            ],
            compiler_params=pltpu.CompilerParams(
                collective_id=0, has_side_effects=True, vmem_limit_bytes=60 << 20),
        )(field, coef, table, inverses, deg, order_ids)
        out = out.reshape(nt, f, c, rd, orders)
        return jnp.transpose(out, (4, 0, 1, 2, 3))

    in_specs = (
        P(None, "row", None, None, "col"),
        P("row", "col"),
        P("row", None, None),
        P("row"),
        P(("row", "col"), None, None),
        P(),
    )
    return jax.shard_map(
        per_device, mesh=mesh, in_specs=in_specs,
        out_specs=P(None, "row", None, None, "col"), check_vma=False)
```

```python
import functools

import jax
import jax.numpy as jnp
from jax import lax
from jax.experimental import pallas as pl
from jax.experimental.pallas import tpu as pltpu
from jax.sharding import PartitionSpec as P

MESH = pl.DeviceIdType.MESH
BF = jnp.bfloat16
F32 = jnp.float32


class Plan:
    def __init__(self, rows, cols, lat, radii, members):
        self.rows, self.cols = rows, cols
        self.co = 2
        self.xl = 4 if rows % 32 == 0 else 2
        self.y = rows // (self.xl * self.co)
        self.na = self.y * self.co
        self.nb = cols * self.xl
        self.deg = rows * cols
        self.t = lat // rows
        self.rd = radii // cols
        self.fc = members
        self.j = members * self.rd


def one_hot(hit):
    return jnp.where(hit, 1.0, 0.0).astype(F32).astype(BF)


def iota(shape, dim):
    return lax.broadcasted_iota(jnp.int32, shape, dim)


def kernel(pn, field, coef, table, inv, deg, order, out,
           fv, cv, tv, iv, dv, s1, r1, sf, perm, tp, tt, w, sp, e1, e2, d2, o2,
           g1, g2, h1, ob, insem, ssem, rsem):
    rows, cols, na, nb, nt, nj = pn.rows, pn.cols, pn.na, pn.nb, pn.t, pn.j
    ny, nx, nc, n_deg = pn.y, pn.xl, pn.co, pn.deg
    me_row, me_col = lax.axis_index("row"), lax.axis_index("col")
    co = me_row % nc
    xl = (me_row // nc) % nx
    y = me_row // (nc * nx)
    me_a = co * ny + y
    me_b = xl * cols + me_col
    u = nt // 8

    def row_dev(k):
        return (k, me_col)

    def a_dev(a):
        return (((a % ny) * nx + xl) * nc + a // ny, me_col)

    def b_dev(b):
        return ((y * nx + b // cols) * nc + co, b % cols)

    loads = [(field, fv), (coef, cv), (deg, dv), (table, tv), (inv, iv)]
    loads = [pltpu.make_async_copy(src, dst, insem.at[i]) for i, (src, dst) in enumerate(loads)]
    for c in loads:
        c.start()

    barrier = pltpu.get_barrier_semaphore()

    def greet_row(s, _):
        pl.semaphore_signal(barrier, inc=1, device_id=row_dev((me_row + s) % rows), device_id_type=MESH)
        return 0

    def greet_b(s, _):
        pl.semaphore_signal(barrier, inc=1, device_id=b_dev((me_b + s) % nb), device_id_type=MESH)
        return 0

    lax.fori_loop(1, rows, greet_row, 0)
    lax.fori_loop(1, nb, greet_b, 0)

    def put(src, dst, stage, half, dev, own):
        @pl.when(own)
        def _():
            pltpu.make_async_copy(src, dst, rsem.at[stage, half]).start()

        @pl.when(jnp.logical_not(own))
        def _():
            pltpu.make_async_remote_copy(
                src_ref=src, dst_ref=dst, send_sem=ssem.at[stage, half], recv_sem=rsem.at[stage, half],
                device_id=dev, device_id_type=MESH).start()

    def arrived(buf, stage, half):
        pltpu.make_async_copy(buf, buf, rsem.at[stage, half]).wait()

    def sent(part, stage, half):
        pltpu.make_async_copy(part, part, ssem.at[stage, half]).wait()

    loads[0].wait()
    loads[1].wait()
    eye = one_hot(iota((rows, rows), 0) == iota((rows, rows), 1))
    tc = 4
    for i in range(nt // tc):
        x = fv[pl.ds(i * tc, tc)].reshape(tc * nj, rows)
        yv = lax.dot_general(eye, x, (((1,), (1,)), ((), ())), preferred_element_type=F32)
        for t in range(tc):
            sf[pl.ds((i * tc + t) * rows, rows), :] = yv[:, t * nj:(t + 1) * nj]
    c4 = jnp.concatenate([cv[...]] * pn.fc, axis=1)
    pl.semaphore_wait(barrier, rows - 1 + nb - 1)
    chips = rows // nc

    for h in range(nc):
        def weigh(s, _):
            k = (me_row // nc + s) % chips * nc + h
            s1[pl.ds(k * u, u)] = (sf[pl.ds(k, nt, stride=rows), :] * c4).astype(BF).reshape(u, 8, nj)
            put(s1.at[pl.ds(k * u, u)], r1.at[pl.ds(me_row * u, u)], 0, 0, row_dev(k), k == me_row)
            return 0

        lax.fori_loop(0, chips, weigh, 0)

    loads[2].wait()
    lanes = min(128, n_deg)
    owner = jnp.broadcast_to(dv[...].reshape(1, n_deg), (128, n_deg)).T[:, :lanes]
    owner = jnp.concatenate(
        [owner[((v * nx + i) * nc + h) * cols:((v * nx + i) * nc + h + 1) * cols]
         for h in range(nc) for v in range(ny) for i in range(nx)], axis=0)
    for c in range(n_deg // lanes):
        lane = iota((n_deg, lanes), 1) + c * lanes
        perm[:, c * lanes:(c + 1) * lanes] = one_hot(jnp.logical_and(owner == lane, lane >= order[0]))
    loads[3].wait()
    qb = min(128, n_deg)

    def permute(i, _):
        q = pl.multiple_of(i * qb, qb)
        block = jnp.dot(perm[pl.ds(q, qb), :], tv[0], preferred_element_type=F32).astype(BF)
        tp[pl.ds(q, qb), :] = block
        tt[:, pl.ds(q, qb)] = block.T
        return 0

    lax.fori_loop(0, n_deg // qb, permute, 0)

    loads[4].wait()
    cg = min(4, cols)
    groups = cols // cg
    nr, nn = cg * pn.rd, cg * nj
    n_id, r_id = iota((nr, nn), 1), iota((nr, nn), 0)
    spread = one_hot(r_id == (n_id // nj) * pn.rd + n_id % pn.rd)
    fc_id = (iota((1, nn), 1) % nj) // pn.rd

    def widen(g, _):
        part = iv[0, pl.ds(pl.multiple_of(g * nr, nr), nr), :]
        x = lax.dot_general(part, spread, (((0,), (0,)), ((), ())), preferred_element_type=F32)
        for f in range(pn.fc):
            z = jnp.where(fc_id == f, x, 0.0).astype(BF)
            w[:, f, :, pl.ds(pl.multiple_of(g * nn, nn), nn)] = z.reshape(cols, pn.rd, nn)
        return 0

    lax.fori_loop(0, groups, widen, 0)

    arrived(r1, 0, 0)
    columns = r1[...].reshape(rows * nt, nj)
    for h in range(nc):
        block = jnp.dot(tp[pl.ds(h * ny * nb, ny * nb), :], columns, preferred_element_type=F32)
        sp[pl.ds(h * ny, ny)] = block.astype(BF).reshape(ny, nb, nj)

        def send_a(s, _):
            a = (y + s) % ny + h * ny
            for half in range(nc):
                @pl.when(co == half)
                def _():
                    put(sp.at[a], e1.at[me_a], 1, half, a_dev(a), a == me_a)
            return 0

        lax.fori_loop(0, ny, send_a, 0)

    for h in range(nc):
        arrived(e1.at[pl.ds(h * ny, ny)], 1, h)
        sf[pl.ds(0, ny * nb), :] = e1[pl.ds(h * ny, ny)].reshape(ny * nb, nj).astype(F32)
        corner = d2.at[h, xl, :, pl.ds(pl.multiple_of(me_col * nj, nj), nj)]

        def send_b(s, _):
            b = (me_b + s) % nb
            e2[h, b] = sf[pl.ds(b, ny, stride=nb), :].astype(BF)
            put(e2.at[h, b], corner, 2, h, b_dev(b), b == me_b)
            return 0

        lax.fori_loop(0, nb, send_b, 0)

    for h in range(nc):
        arrived(d2.at[h], 2, h)
        left = d2[h].reshape(nx * ny, cols * nj)
        for i in range(groups):
            g = (me_col // cg + i) % groups
            span = pl.ds(pl.multiple_of(g * nn, nn), nn)
            right = w[:, :, :, span].reshape(cols * nj, nn)
            part = jnp.dot(left, right, preferred_element_type=F32).astype(BF)
            o2[h, :, :, span] = part.reshape(nx, ny, nn)

            def send_back(s, _):
                xd = (xl + s // cg) % nx
                cd = g * cg + (me_col + s) % cg
                src = o2.at[h, xd, :, pl.ds(pl.multiple_of(cd * nj, nj), nj)]
                b = xd * cols + cd
                put(src, g1.at[h, me_b], 3, h, b_dev(b), b == me_b)
                return 0

            lax.fori_loop(0, nx * cg, send_back, 0)

    for h in range(nc):
        arrived(g1.at[h], 3, h)
        sf[pl.ds(0, ny * nb), :] = g1[h].reshape(ny * nb, nj).astype(F32)

        def send_home(s, _):
            v = (y + s) % ny
            a = h * ny + v
            g2[a] = sf[pl.ds(v, nb, stride=ny), :].astype(BF)
            put(g2.at[a], h1.at[me_a], 4, 0, a_dev(a), a == me_a)
            return 0

        lax.fori_loop(0, ny, send_home, 0)

    arrived(h1, 4, 0)
    coeffs = h1[...].reshape(n_deg, nj)
    parts = 4
    kg = rows // parts
    lg = kg * nt
    for i in range(parts):
        g = (me_row // kg + i) % parts
        rows_of = pl.ds(pl.multiple_of(g * lg, lg), lg)
        block = jnp.dot(tt[rows_of, :], coeffs, preferred_element_type=F32)
        ob[pl.ds(g * (lg // 8), lg // 8)] = block.astype(BF).reshape(lg // 8, 8, nj)

        def send_out(s, _):
            k = g * kg + (me_row + s) % kg
            put(ob.at[pl.ds(k * u, u)], out.at[pl.ds(me_row * u, u)], 5, 0, row_dev(k), k == me_row)
            return 0

        lax.fori_loop(0, kg, send_out, 0)

    sent(s1.at[pl.ds(0, (rows - 1) * u)], 0, 0)
    for half in range(nc):
        @pl.when(co == half)
        def _():
            sent(sp.at[pl.ds(0, na - 1)], 1, half)
        sent(e2.at[half, pl.ds(0, nb - 1)], 2, half)
        sent(g1.at[half, pl.ds(0, nb - 1)], 3, half)
    sent(g2.at[pl.ds(0, na - 1)], 4, 0)
    sent(ob.at[pl.ds(0, (rows - 1) * u)], 5, 0)
    arrived(out, 5, 0)


def unfold(v, out, sf):
    rows, _, nt, nj = v.shape
    sf[...] = v[:, 0].reshape(rows * nt, nj).astype(F32)
    eye = one_hot(iota((nj, nj), 0) == iota((nj, nj), 1))
    for t in range(nt):
        z = sf[pl.ds(t, rows, stride=nt), :].astype(BF)
        out[t] = lax.dot_general(eye, z, (((1,), (1,)), ((), ())), preferred_element_type=F32).astype(BF)


def solution(mesh):
    rows, cols = mesh.shape["row"], mesh.shape["col"]

    def per_device(field, coef, table, order_ids, inverses, degree_owner):
        orders, nt, f, c, rd = field.shape
        pn = Plan(rows, cols, table.shape[2], rd * cols, f * c)
        na, nb, nj, n_deg = pn.na, pn.nb, pn.j, pn.deg
        lat = rows * nt
        field = jnp.transpose(field, (1, 2, 3, 4, 0)).reshape(nt, nj, orders)
        anyspace = pl.BlockSpec(memory_space=pl.ANY)
        half = (pn.co, pn.xl, pn.y, cols * nj)
        out = pl.pallas_call(
            functools.partial(kernel, pn),
            out_shape=jax.ShapeDtypeStruct((lat // 8, 8, nj), BF),
            in_specs=[anyspace] * 5 + [pl.BlockSpec(memory_space=pltpu.SMEM)],
            out_specs=anyspace,
            scratch_shapes=[
                pltpu.VMEM((nt, nj, orders), BF),
                pltpu.VMEM((nt, rd), F32),
                pltpu.VMEM((1, n_deg, lat), BF),
                pltpu.VMEM((1, cols * rd, cols * rd), BF),
                pltpu.VMEM((n_deg,), jnp.int32),
                pltpu.VMEM((lat // 8, 8, nj), BF),
                pltpu.VMEM((lat // 8, 8, nj), BF),
                pltpu.VMEM((lat, nj), F32),
                pltpu.VMEM((n_deg, n_deg), BF),
                pltpu.VMEM((n_deg, lat), BF),
                pltpu.VMEM((lat, n_deg), BF),
                pltpu.VMEM((cols, pn.fc, rd, cols * nj), BF),
                pltpu.VMEM((na, nb, nj), BF),
                pltpu.VMEM((na, nb, nj), BF),
                pltpu.VMEM((pn.co, nb, pn.y, nj), BF),
                pltpu.VMEM(half, BF),
                pltpu.VMEM(half, BF),
                pltpu.VMEM((pn.co, nb, pn.y, nj), BF),
                pltpu.VMEM((na, nb, nj), BF),
                pltpu.VMEM((na, nb, nj), BF),
                pltpu.VMEM((lat // 8, 8, nj), BF),
                pltpu.SemaphoreType.DMA((5,)),
                pltpu.SemaphoreType.DMA((6, 2)),
                pltpu.SemaphoreType.DMA((6, 2)),
            ],
            compiler_params=pltpu.CompilerParams(
                collective_id=0, has_side_effects=True, vmem_limit_bytes=60 << 20),
        )(field, coef, table, inverses, degree_owner, order_ids)
        out = pl.pallas_call(
            unfold,
            grid=(nt // 8,),
            out_shape=jax.ShapeDtypeStruct((nt, nj, orders), BF),
            in_specs=[pl.BlockSpec((orders, 1, 8, nj), lambda i: (0, i, 0, 0))],
            out_specs=pl.BlockSpec((8, nj, orders), lambda i: (i, 0, 0)),
            scratch_shapes=[pltpu.VMEM((orders * 8, nj), F32)],
        )(out.reshape(orders, nt // 8, 8, nj))
        out = out.reshape(nt, f, c, rd, orders)
        return jnp.transpose(out, (4, 0, 1, 2, 3))

    in_specs = (
        P(None, "row", None, None, "col"),
        P("row", "col"),
        P("row", None, None),
        P("row"),
        P(("row", "col"), None, None),
        P(),
    )
    return jax.shard_map(
        per_device, mesh=mesh, in_specs=in_specs,
        out_specs=P(None, "row", None, None, "col"), check_vma=False)
```

```python
import functools

import jax
import jax.numpy as jnp
from jax import lax
from jax.experimental import pallas as pl
from jax.experimental.pallas import tpu as pltpu
from jax.sharding import PartitionSpec as P

MESH = pl.DeviceIdType.MESH
BF = jnp.bfloat16
F32 = jnp.float32


class Plan:
    def __init__(self, rows, cols, lat, radii, members):
        self.rows, self.cols = rows, cols
        self.co = 2
        self.xl = 4 if rows % 32 == 0 else 2
        self.y = rows // (self.xl * self.co)
        self.na = self.y * self.co
        self.nb = cols * self.xl
        self.deg = rows * cols
        self.t = lat // rows
        self.rd = radii // cols
        self.fc = members
        self.j = members * self.rd


def one_hot(hit):
    return jnp.where(hit, 1.0, 0.0).astype(F32).astype(BF)


def iota(shape, dim):
    return lax.broadcasted_iota(jnp.int32, shape, dim)


def wrap(i, n):
    return jnp.where(i >= n, i - n, i)


def far(t, n):
    return jnp.where(t % 2 == 1, n // 2 - (t + 1) // 2, n // 2 + t // 2)


def far_list(n):
    return [n // 2 - (t + 1) // 2 if t % 2 else n // 2 + t // 2 for t in range(n)]


def regroup(blocks, width):
    n = len(blocks)
    group = iota((1, blocks[0].shape[1]), 1) // width
    out = []
    for f in range(n):
        moved = [pltpu.roll(x, (p - f) % n * width, 1) if p != f else x for p, x in enumerate(blocks)]
        y = moved[0]
        for p in range(1, n):
            y = jnp.where(group == p, moved[p], y)
        out.append(y)
    return out


def kernel(pn, field, coef, table, inv, deg, order, out,
           fv, cv, tv, iv, dv, s1, r1, sf, perm, tp, tt, w, sp, e1, e2, d2, o2,
           g1, g2, h1, ob, insem, ssem, rsem):
    rows, cols, na, nb, nt, nj = pn.rows, pn.cols, pn.na, pn.nb, pn.t, pn.j
    ny, nx, nc, n_deg = pn.y, pn.xl, pn.co, pn.deg
    me_row, me_col = lax.axis_index("row"), lax.axis_index("col")
    co = me_row % nc
    xl = (me_row // nc) % nx
    y = me_row // (nc * nx)
    me_a = co * ny + y
    me_b = xl * cols + me_col
    u = nt // 8

    loads = [(field, fv), (coef, cv), (deg, dv), (table, tv), (inv, iv)]
    loads = [pltpu.make_async_copy(src, dst, insem.at[i]) for i, (src, dst) in enumerate(loads)]
    for c in loads:
        c.start()

    barrier = pltpu.get_barrier_semaphore()

    def greet(dev):
        pl.semaphore_signal(barrier, inc=1, device_id=dev, device_id_type=MESH)

    nz, ring = cols // 2, 2 * nx
    x8 = me_col % 2 * nx + xl
    z = me_col // 2
    across = []
    for dx in far_list(ring):
        xd = wrap(x8 + dx, ring)
        across.append((xd % nx, xd // nx, (y * nx + xd % nx) * nc + co))
    others = [wrap(xl + i, nx) for i in range(nx)]
    lines = [(y * nx + xd) * nc + co for xd in others]
    chips = rows // nc
    chip = y * nx + xl

    greet((chip * nc + 1 - co, me_col))

    def greet_row(s, _):
        k = wrap(chip + s, chips) * nc
        for h in range(nc):
            greet((k + h, me_col))
        return 0

    lax.fori_loop(1, chips, greet_row, 0)
    for line in lines[1:]:
        greet((line, me_col))

    def greet_b(j, _):
        cd = wrap(me_col + j, cols)
        for line in lines:
            greet((line, cd))
        return 0

    lax.fori_loop(1, cols, greet_b, 0)

    def put(src, dst, stage, half, dev):
        pltpu.make_async_remote_copy(
            src_ref=src, dst_ref=dst, send_sem=ssem.at[stage, half], recv_sem=rsem.at[stage, half],
            device_id=dev, device_id_type=MESH).start()

    def keep(src, dst, stage, half):
        pltpu.make_async_copy(src, dst, rsem.at[stage, half]).start()

    def arrived(buf, stage, half):
        pltpu.make_async_copy(buf, buf, rsem.at[stage, half]).wait()

    def sent(part, stage, half):
        pltpu.make_async_copy(part, part, ssem.at[stage, half]).wait()

    loads[0].wait()
    loads[1].wait()
    eye = one_hot(iota((rows, rows), 0) == iota((rows, rows), 1))
    tc = 4
    for i in range(nt // tc):
        x = fv[pl.ds(i * tc, tc)].reshape(tc * nj, rows)
        yv = lax.dot_general(eye, x, (((1,), (1,)), ((), ())), preferred_element_type=F32)
        for t in range(tc):
            sf[pl.ds((i * tc + t) * rows, rows), :] = yv[:, t * nj:(t + 1) * nj]
    c4 = jnp.concatenate([cv[...]] * pn.fc, axis=1)
    pl.semaphore_wait(barrier, rows - 1 + nb - 1)

    def weigh(k):
        block = (sf[pl.ds(k, nt, stride=rows), :] * c4).astype(BF)
        s1[pl.ds(k * u, u)] = block.reshape(u, 8, nj)
        return s1.at[pl.ds(k * u, u)], r1.at[pl.ds(me_row * u, u)], 0, 0

    def weigh_half(h):
        def weigh_all(t, _):
            v = wrap(y + far(t, ny), ny)
            for xd in others:
                k = (v * nx + xd) * nc + h
                put(*weigh(k), (k, me_col))
            return 0

        lax.fori_loop(0, ny - 1, weigh_all, 0)
        for xd in others[1:]:
            k = (y * nx + xd) * nc + h
            put(*weigh(k), (k, me_col))

        @pl.when(co == h)
        def _():
            keep(*weigh(me_row))

        @pl.when(co != h)
        def _():
            k = chip * nc + h
            put(*weigh(k), (k, me_col))

    weigh_half(0)

    loads[2].wait()
    lanes = min(128, n_deg)
    owner = jnp.broadcast_to(dv[...].reshape(1, n_deg), (128, n_deg)).T[:, :lanes]
    owner = jnp.concatenate(
        [owner[((v * nx + i) * nc + h) * cols:((v * nx + i) * nc + h + 1) * cols]
         for h in range(nc) for v in range(ny) for i in range(nx)], axis=0)
    for c in range(n_deg // lanes):
        lane = iota((n_deg, lanes), 1) + c * lanes
        perm[:, c * lanes:(c + 1) * lanes] = one_hot(jnp.logical_and(owner == lane, lane >= order[0]))
    loads[3].wait()
    qb = min(512, n_deg)

    def permute(i, _):
        q = pl.multiple_of(i * qb, qb)
        tp[pl.ds(q, qb), :] = jnp.dot(perm[pl.ds(q, qb), :], tv[0], preferred_element_type=F32).astype(BF)
        return 0

    lax.fori_loop(0, 1, permute, 0)
    for h in range(1, nc):
        weigh_half(h)
    lax.fori_loop(1, n_deg // qb, permute, 0)

    loads[4].wait()
    tb = min(256, n_deg)

    def turn(i, _):
        q = pl.multiple_of(i * tb, tb)
        tt[:, pl.ds(q, tb)] = tp[pl.ds(q, tb), :].T
        return 0

    def prepare():
        w[...] = iv[0].T
        lax.fori_loop(0, n_deg // tb, turn, 0)

    @pl.when(co != 0)
    def _():
        prepare()

    arrived(r1, 0, 0)
    columns = r1[...].reshape(rows * nt, nj)
    for h in range(nc):
        block = jnp.dot(tp[pl.ds(h * ny * nb, ny * nb), :], columns, preferred_element_type=F32)
        sp[pl.ds(h * ny, ny)] = block.astype(BF).reshape(ny, nb, nj)

        for half in range(nc):
            @pl.when(co == half)
            def _():
                def send_a(v, h=h, half=half):
                    a = h * ny + v
                    return sp.at[a], e1.at[me_a], 1, half

                def send_all(t, _):
                    v = wrap(y + far(t, ny), ny)
                    put(*send_a(v), ((v * nx + xl) * nc + h, me_col))
                    return 0

                lax.fori_loop(0, ny - 1, send_all, 0)
                if half == h:
                    keep(*send_a(y))
                else:
                    put(*send_a(y), (chip * nc + h, me_col))

    @pl.when(co == 0)
    def _():
        prepare()

    def to_b(block):
        def line_of(t, _):
            zd = wrap(z + far(t, nz), nz) * 2
            for xd, hi, line in across:
                put(*block(xd * cols + zd + hi), (line, zd + hi))
            return 0

        lax.fori_loop(0, nz - 1, line_of, 0)
        for xd, hi, line in across[:-1]:
            put(*block(xd * cols + z * 2 + hi), (line, z * 2 + hi))
        keep(*block(me_b))

    for h in range(nc):
        arrived(e1.at[pl.ds(h * ny, ny)], 1, h)
        sf[pl.ds(0, ny * nb), :] = e1[pl.ds(h * ny, ny)].reshape(ny * nb, nj).astype(F32)
        corner = d2.at[h, xl, :, pl.ds(pl.multiple_of(me_col * nj, nj), nj)]

        def send_b(b):
            e2[h, b] = sf[pl.ds(b, ny, stride=nb), :].astype(BF)
            return e2.at[h, b], corner, 2, h

        to_b(send_b)

    for h in range(nc):
        arrived(d2.at[h], 2, h)
        left = d2[h].reshape(nx * ny, cols * nj).astype(F32)
        fc, m = pn.fc, nx * ny
        quads = [regroup([left[:, (g * fc + p) * nj:(g * fc + p + 1) * nj] for p in range(fc)], pn.rd)
                 for g in range(cols // fc)]
        left = jnp.concatenate(
            [jnp.concatenate([quad[f] for quad in quads], axis=1) for f in range(fc)], axis=0).astype(BF)
        right = jnp.dot(left, w[...], preferred_element_type=F32)
        for g in range(cols // fc):
            quad = regroup([right[f * m:(f + 1) * m, g * nj:(g + 1) * nj] for f in range(fc)], pn.rd)
            for p in range(fc):
                c = g * fc + p
                o2[h, :, :, c * nj:(c + 1) * nj] = quad[p].astype(BF).reshape(nx, ny, nj)

        def send_back(b, h=h):
            src = o2.at[h, b // cols, :, pl.ds(pl.multiple_of(b % cols * nj, nj), nj)]
            return src, g1.at[h, me_b], 3, h

        to_b(send_back)

    for h in range(nc):
        arrived(g1.at[h], 3, h)
        sf[pl.ds(0, ny * nb), :] = g1[h].reshape(ny * nb, nj).astype(F32)

        def send_home(v, h=h):
            a = h * ny + v
            g2[a] = sf[pl.ds(v, nb, stride=ny), :].astype(BF)
            return g2.at[a], h1.at[me_a], 4, 0

        def send_homes(t, _):
            v = wrap(y + far(t, ny), ny)
            put(*send_home(v), ((v * nx + xl) * nc + h, me_col))
            return 0

        lax.fori_loop(0, ny - 1, send_homes, 0)

        @pl.when(co == h)
        def _():
            keep(*send_home(y))

        @pl.when(co != h)
        def _():
            put(*send_home(y), (chip * nc + h, me_col))

    arrived(h1, 4, 0)
    coeffs = h1[...].reshape(n_deg, nj)
    parts = 4
    kg = rows // parts
    lg = kg * nt
    for i in far_list(parts):
        g = wrap(me_row // kg + i, parts)
        rows_of = pl.ds(pl.multiple_of(g * lg, lg), lg)
        block = jnp.dot(tt[rows_of, :], coeffs, preferred_element_type=F32)
        ob[pl.ds(g * (lg // 8), lg // 8)] = block.astype(BF).reshape(lg // 8, 8, nj)

        def send_out(k):
            return ob.at[pl.ds(k * u, u)], out.at[pl.ds(me_row * u, u)], 5, 0

        first = me_row % kg
        if i == 0:
            keep(*send_out(me_row))
        else:
            put(*send_out(g * kg + first), (g * kg + first, me_col))

        def send_outs(s, _):
            k = g * kg + wrap(first + s, kg)
            put(*send_out(k), (k, me_col))
            return 0

        lax.fori_loop(1, kg, send_outs, 0)

    arrived(out, 5, 0)
    sent(s1.at[pl.ds(0, (rows - 1) * u)], 0, 0)
    for half in range(nc):
        @pl.when(co == half)
        def _():
            sent(sp.at[pl.ds(0, na - 1)], 1, half)
        sent(e2.at[half, pl.ds(0, nb - 1)], 2, half)
        sent(g1.at[half, pl.ds(0, nb - 1)], 3, half)
    sent(g2.at[pl.ds(0, na - 1)], 4, 0)
    sent(ob.at[pl.ds(0, (rows - 1) * u)], 5, 0)


def unfold(v, out, sf):
    rows, _, nt, nj = v.shape
    sf[...] = v[:, 0].reshape(rows * nt, nj).astype(F32)
    eye = one_hot(iota((nj, nj), 0) == iota((nj, nj), 1))
    for t in range(nt):
        z = sf[pl.ds(t, rows, stride=nt), :].astype(BF)
        out[t] = lax.dot_general(eye, z, (((1,), (1,)), ((), ())), preferred_element_type=F32).astype(BF)


def solution(mesh):
    rows, cols = mesh.shape["row"], mesh.shape["col"]

    def per_device(field, coef, table, order_ids, inverses, degree_owner):
        orders, nt, f, c, rd = field.shape
        pn = Plan(rows, cols, table.shape[2], rd * cols, f * c)
        na, nb, nj, n_deg = pn.na, pn.nb, pn.j, pn.deg
        lat = rows * nt
        field = jnp.transpose(field, (1, 2, 3, 4, 0)).reshape(nt, nj, orders)
        anyspace = pl.BlockSpec(memory_space=pl.ANY)
        half = (pn.co, pn.xl, pn.y, cols * nj)
        out = pl.pallas_call(
            functools.partial(kernel, pn),
            out_shape=jax.ShapeDtypeStruct((lat // 8, 8, nj), BF),
            in_specs=[anyspace] * 5 + [pl.BlockSpec(memory_space=pltpu.SMEM)],
            out_specs=anyspace,
            scratch_shapes=[
                pltpu.VMEM((nt, nj, orders), BF),
                pltpu.VMEM((nt, rd), F32),
                pltpu.VMEM((1, n_deg, lat), BF),
                pltpu.VMEM((1, cols * rd, cols * rd), BF),
                pltpu.VMEM((n_deg,), jnp.int32),
                pltpu.VMEM((lat // 8, 8, nj), BF),
                pltpu.VMEM((lat // 8, 8, nj), BF),
                pltpu.VMEM((lat, nj), F32),
                pltpu.VMEM((n_deg, n_deg), BF),
                pltpu.VMEM((n_deg, lat), BF),
                pltpu.VMEM((lat, n_deg), BF),
                pltpu.VMEM((cols * rd, cols * rd), BF),
                pltpu.VMEM((na, nb, nj), BF),
                pltpu.VMEM((na, nb, nj), BF),
                pltpu.VMEM((pn.co, nb, pn.y, nj), BF),
                pltpu.VMEM(half, BF),
                pltpu.VMEM(half, BF),
                pltpu.VMEM((pn.co, nb, pn.y, nj), BF),
                pltpu.VMEM((na, nb, nj), BF),
                pltpu.VMEM((na, nb, nj), BF),
                pltpu.VMEM((lat // 8, 8, nj), BF),
                pltpu.SemaphoreType.DMA((5,)),
                pltpu.SemaphoreType.DMA((6, 2)),
                pltpu.SemaphoreType.DMA((6, 2)),
            ],
            compiler_params=pltpu.CompilerParams(
                collective_id=0, has_side_effects=True, vmem_limit_bytes=60 << 20),
        )(field, coef, table, inverses, degree_owner, order_ids)
        out = pl.pallas_call(
            unfold,
            grid=(nt // 8,),
            out_shape=jax.ShapeDtypeStruct((nt, nj, orders), BF),
            in_specs=[pl.BlockSpec((orders, 1, 8, nj), lambda i: (0, i, 0, 0))],
            out_specs=pl.BlockSpec((8, nj, orders), lambda i: (i, 0, 0)),
            scratch_shapes=[pltpu.VMEM((orders * 8, nj), F32)],
        )(out.reshape(orders, nt // 8, 8, nj))
        out = out.reshape(nt, f, c, rd, orders)
        return jnp.transpose(out, (4, 0, 1, 2, 3))

    in_specs = (
        P(None, "row", None, None, "col"),
        P("row", "col"),
        P("row", None, None),
        P("row"),
        P(("row", "col"), None, None),
        P(),
    )
    return jax.shard_map(
        per_device, mesh=mesh, in_specs=in_specs,
        out_specs=P(None, "row", None, None, "col"), check_vma=False)
```

```python
import functools

import jax
import jax.numpy as jnp
from jax import lax
from jax.experimental import pallas as pl
from jax.experimental.pallas import tpu as pltpu
from jax.sharding import PartitionSpec as P

MESH = pl.DeviceIdType.MESH
BF = jnp.bfloat16
F32 = jnp.float32


class Plan:
    def __init__(self, rows, cols, lat, radii, members):
        self.rows, self.cols = rows, cols
        self.co = 2
        self.xl = 4 if rows % 32 == 0 else 2
        self.y = rows // (self.xl * self.co)
        self.na = self.y * self.co
        self.nb = cols * self.xl
        self.deg = rows * cols
        self.t = lat // rows
        self.rd = radii // cols
        self.fc = members
        self.j = members * self.rd


def one_hot(hit):
    return jnp.where(hit, 1.0, 0.0).astype(F32).astype(BF)


def iota(shape, dim):
    return lax.broadcasted_iota(jnp.int32, shape, dim)


def wrap(i, n):
    return jnp.where(i >= n, i - n, i)


def far(t, n):
    return jnp.where(t % 2 == 1, n // 2 - (t + 1) // 2, n // 2 + t // 2)


def far_list(n):
    return [n // 2 - (t + 1) // 2 if t % 2 else n // 2 + t // 2 for t in range(n)]


def regroup(blocks, width):
    n = len(blocks)
    group = iota((1, blocks[0].shape[1]), 1) // width
    out = []
    for f in range(n):
        moved = [pltpu.roll(x, (p - f) % n * width, 1) if p != f else x for p, x in enumerate(blocks)]
        y = moved[0]
        for p in range(1, n):
            y = jnp.where(group == p, moved[p], y)
        out.append(y)
    return out


def kernel(pn, field, coef, table, inv, deg, order, out,
           fv, cv, tv, iv, dv, s1, r1, sf, perm, tp, tt, w, sp, e1, e2, d2, o2,
           g1, g2, h1, ob, ov, insem, ssem, rsem):
    rows, cols, na, nb, nt, nj = pn.rows, pn.cols, pn.na, pn.nb, pn.t, pn.j
    ny, nx, nc, n_deg = pn.y, pn.xl, pn.co, pn.deg
    me_row, me_col = lax.axis_index("row"), lax.axis_index("col")
    co = me_row % nc
    xl = (me_row // nc) % nx
    y = me_row // (nc * nx)
    me_a = co * ny + y
    me_b = xl * cols + me_col
    u = nt // 8

    loads = [(field, fv), (coef, cv), (deg, dv), (table, tv), (inv, iv), (order, ov)]
    loads = [pltpu.make_async_copy(src, dst, insem.at[i]) for i, (src, dst) in enumerate(loads)]
    for c in loads:
        c.start()

    barrier = pltpu.get_barrier_semaphore()

    def greet(dev):
        pl.semaphore_signal(barrier, inc=1, device_id=dev, device_id_type=MESH)

    nz, ring = cols // 2, 2 * nx
    x8 = me_col % 2 * nx + xl
    z = me_col // 2
    across = []
    for dx in far_list(ring):
        xd = wrap(x8 + dx, ring)
        across.append((xd % nx, xd // nx, (y * nx + xd % nx) * nc + co))
    others = [wrap(xl + i, nx) for i in range(nx)]
    chip = y * nx + xl

    def greet_b(t, _):
        zd = wrap(z + far(t, nz), nz) * 2
        for _, hi, line in across:
            greet((line, zd + hi))
        return 0

    def greet_row(t, _):
        v = wrap(y + far(t, ny), ny)
        for xd in others:
            for h in range(nc):
                greet(((v * nx + xd) * nc + h, me_col))
        return 0

    lax.fori_loop(0, nz - 1, greet_b, 0)
    lax.fori_loop(0, ny - 1, greet_row, 0)
    for _, hi, line in across[:-1]:
        greet((line, z * 2 + hi))
    for xd in others[1:]:
        for h in range(nc):
            greet(((y * nx + xd) * nc + h, me_col))
    greet((chip * nc + 1 - co, me_col))

    def put(src, dst, stage, half, dev):
        pltpu.make_async_remote_copy(
            src_ref=src, dst_ref=dst, send_sem=ssem.at[stage, half], recv_sem=rsem.at[stage, half],
            device_id=dev, device_id_type=MESH).start()

    def keep(src, dst, stage, half):
        pltpu.make_async_copy(src, dst, rsem.at[stage, half]).start()

    def arrived(buf, stage, half):
        pltpu.make_async_copy(buf, buf, rsem.at[stage, half]).wait()

    def sent(part, stage, half):
        pltpu.make_async_copy(part, part, ssem.at[stage, half]).wait()

    loads[0].wait()
    loads[1].wait()
    eye = one_hot(iota((rows, rows), 0) == iota((rows, rows), 1))
    tc = 4
    for i in range(nt // tc):
        x = fv[pl.ds(i * tc, tc)].reshape(tc * nj, rows)
        yv = lax.dot_general(eye, x, (((1,), (1,)), ((), ())), preferred_element_type=F32)
        for t in range(tc):
            sf[pl.ds((i * tc + t) * rows, rows), :] = yv[:, t * nj:(t + 1) * nj]
    c4 = jnp.concatenate([cv[...]] * pn.fc, axis=1)
    pl.semaphore_wait(barrier, rows - 1 + nb - 1)

    def weigh(k):
        block = (sf[pl.ds(k, nt, stride=rows), :] * c4).astype(BF)
        s1[pl.ds(k * u, u)] = block.reshape(u, 8, nj)
        return s1.at[pl.ds(k * u, u)], r1.at[pl.ds(me_row * u, u)], 0, 0

    def weigh_half(h):
        def weigh_all(t, _):
            v = wrap(y + far(t, ny), ny)
            for xd in others:
                k = (v * nx + xd) * nc + h
                put(*weigh(k), (k, me_col))
            return 0

        lax.fori_loop(0, ny - 1, weigh_all, 0)
        for xd in others[1:]:
            k = (y * nx + xd) * nc + h
            put(*weigh(k), (k, me_col))

        @pl.when(co == h)
        def _():
            keep(*weigh(me_row))

        @pl.when(co != h)
        def _():
            k = chip * nc + h
            put(*weigh(k), (k, me_col))

    weigh_half(0)

    loads[2].wait()
    loads[5].wait()
    lanes = min(128, n_deg)
    owner = jnp.broadcast_to(dv[...].reshape(1, n_deg), (128, n_deg)).T[:, :lanes]
    owner = jnp.concatenate(
        [owner[((v * nx + i) * nc + h) * cols:((v * nx + i) * nc + h + 1) * cols]
         for h in range(nc) for v in range(ny) for i in range(nx)], axis=0)
    for c in range(n_deg // lanes):
        lane = iota((n_deg, lanes), 1) + c * lanes
        perm[:, c * lanes:(c + 1) * lanes] = one_hot(jnp.logical_and(owner == lane, lane >= ov[0]))
    loads[3].wait()
    qb = min(512, n_deg)

    def permute(i, _):
        q = pl.multiple_of(i * qb, qb)
        tp[pl.ds(q, qb), :] = jnp.dot(perm[pl.ds(q, qb), :], tv[0], preferred_element_type=F32).astype(BF)
        return 0

    lax.fori_loop(0, 1, permute, 0)
    for h in range(1, nc):
        weigh_half(h)
    lax.fori_loop(1, n_deg // qb, permute, 0)

    loads[4].wait()
    tb = min(256, n_deg)

    def turn(i, _):
        q = pl.multiple_of(i * tb, tb)
        tt[:, pl.ds(q, tb)] = tp[pl.ds(q, tb), :].T
        return 0

    def prepare():
        w[...] = iv[0].T
        lax.fori_loop(0, n_deg // tb, turn, 0)

    @pl.when(co != 0)
    def _():
        prepare()

    arrived(r1, 0, 0)
    columns = r1[...].reshape(rows * nt, nj)
    for h in range(nc):
        block = jnp.dot(tp[pl.ds(h * ny * nb, ny * nb), :], columns, preferred_element_type=F32)
        sp[pl.ds(h * ny, ny)] = block.astype(BF).reshape(ny, nb, nj)

        for half in range(nc):
            @pl.when(co == half)
            def _():
                def send_a(v, h=h, half=half):
                    a = h * ny + v
                    return sp.at[a], e1.at[me_a], 1, half

                def send_all(t, _):
                    v = wrap(y + far(t, ny), ny)
                    put(*send_a(v), ((v * nx + xl) * nc + h, me_col))
                    return 0

                lax.fori_loop(0, ny - 1, send_all, 0)
                if half == h:
                    keep(*send_a(y))
                else:
                    put(*send_a(y), (chip * nc + h, me_col))

    @pl.when(co == 0)
    def _():
        prepare()

    def to_b(block):
        def line_of(t, _):
            zd = wrap(z + far(t, nz), nz) * 2
            for xd, hi, line in across:
                put(*block(xd * cols + zd + hi), (line, zd + hi))
            return 0

        lax.fori_loop(0, nz - 1, line_of, 0)
        for xd, hi, line in across[:-1]:
            put(*block(xd * cols + z * 2 + hi), (line, z * 2 + hi))
        keep(*block(me_b))

    for h in range(nc):
        arrived(e1.at[pl.ds(h * ny, ny)], 1, h)
        sf[pl.ds(0, ny * nb), :] = e1[pl.ds(h * ny, ny)].reshape(ny * nb, nj).astype(F32)
        corner = d2.at[h, xl, :, pl.ds(pl.multiple_of(me_col * nj, nj), nj)]

        def send_b(b):
            e2[h, b] = sf[pl.ds(b, ny, stride=nb), :].astype(BF)
            return e2.at[h, b], corner, 2, h

        to_b(send_b)

    for h in range(nc):
        arrived(d2.at[h], 2, h)
        left = d2[h].reshape(nx * ny, cols * nj).astype(F32)
        fc, m = pn.fc, nx * ny
        quads = [regroup([left[:, (g * fc + p) * nj:(g * fc + p + 1) * nj] for p in range(fc)], pn.rd)
                 for g in range(cols // fc)]
        left = jnp.concatenate(
            [jnp.concatenate([quad[f] for quad in quads], axis=1) for f in range(fc)], axis=0).astype(BF)
        right = jnp.dot(left, w[...], preferred_element_type=F32)
        for g in range(cols // fc):
            quad = regroup([right[f * m:(f + 1) * m, g * nj:(g + 1) * nj] for f in range(fc)], pn.rd)
            for p in range(fc):
                c = g * fc + p
                o2[h, :, :, c * nj:(c + 1) * nj] = quad[p].astype(BF).reshape(nx, ny, nj)

        def send_back(b, h=h):
            src = o2.at[h, b // cols, :, pl.ds(pl.multiple_of(b % cols * nj, nj), nj)]
            return src, g1.at[h, me_b], 3, h

        to_b(send_back)

    for h in range(nc):
        arrived(g1.at[h], 3, h)
        sf[pl.ds(0, ny * nb), :] = g1[h].reshape(ny * nb, nj).astype(F32)

        for half in range(nc):
            @pl.when(co == half)
            def _():
                def send_home(v, h=h, half=half):
                    a = h * ny + v
                    g2[a] = sf[pl.ds(v, nb, stride=ny), :].astype(BF)
                    return g2.at[a], h1.at[me_a], 4, half

                def send_homes(t, _):
                    v = wrap(y + far(t, ny), ny)
                    put(*send_home(v), ((v * nx + xl) * nc + h, me_col))
                    return 0

                lax.fori_loop(0, ny - 1, send_homes, 0)
                if half == h:
                    keep(*send_home(y))
                else:
                    put(*send_home(y), (chip * nc + h, me_col))

    parts = 4
    kg = rows // parts
    lg = kg * nt
    hq = ny * nb
    arrived(h1.at[pl.ds(0, ny)], 4, 0)
    first = h1[pl.ds(0, ny)].reshape(hq, nj)
    for i in range(parts):
        rows_of = pl.ds(i * lg, lg)
        sf[rows_of, :] = jnp.dot(tt[rows_of, :hq], first, preferred_element_type=F32)
    arrived(h1.at[pl.ds(ny, ny)], 4, 1)
    second = h1[pl.ds(ny, ny)].reshape(hq, nj)
    for i in far_list(parts):
        g = wrap(me_row // kg + i, parts)
        rows_of = pl.ds(pl.multiple_of(g * lg, lg), lg)
        block = sf[rows_of, :] + jnp.dot(tt[rows_of, hq:], second, preferred_element_type=F32)
        ob[pl.ds(g * (lg // 8), lg // 8)] = block.astype(BF).reshape(lg // 8, 8, nj)

        def send_out(k):
            return ob.at[pl.ds(k * u, u)], out.at[pl.ds(me_row * u, u)], 5, 0

        mine = me_row % kg
        if i == 0:
            keep(*send_out(me_row))
        else:
            put(*send_out(g * kg + mine), (g * kg + mine, me_col))

        def send_outs(s, _):
            k = g * kg + wrap(mine + s, kg)
            put(*send_out(k), (k, me_col))
            return 0

        lax.fori_loop(1, kg, send_outs, 0)

    arrived(out, 5, 0)
    sent(s1.at[pl.ds(0, (rows - 1) * u)], 0, 0)
    for half in range(nc):
        @pl.when(co == half)
        def _():
            sent(sp.at[pl.ds(0, na - 1)], 1, half)
            sent(g2.at[pl.ds(0, na - 1)], 4, half)
        sent(e2.at[half, pl.ds(0, nb - 1)], 2, half)
        sent(g1.at[half, pl.ds(0, nb - 1)], 3, half)
    sent(ob.at[pl.ds(0, (rows - 1) * u)], 5, 0)


def unfold(v, out, sf):
    rows, _, _, nj = v.shape
    nt = out.shape[0]
    sf[...] = v[...].reshape(rows * nt, nj).astype(F32)
    for t in range(nt):
        out[t] = sf[pl.ds(t, rows, stride=nt), :].T.astype(BF)


def solution(mesh):
    rows, cols = mesh.shape["row"], mesh.shape["col"]

    def per_device(field, coef, table, order_ids, inverses, degree_owner):
        orders, nt, f, c, rd = field.shape
        pn = Plan(rows, cols, table.shape[2], rd * cols, f * c)
        na, nb, nj, n_deg = pn.na, pn.nb, pn.j, pn.deg
        lat = rows * nt
        field = jnp.transpose(field, (1, 2, 3, 4, 0)).reshape(nt, nj, orders)
        anyspace = pl.BlockSpec(memory_space=pl.ANY)
        half = (pn.co, pn.xl, pn.y, cols * nj)
        out = pl.pallas_call(
            functools.partial(kernel, pn),
            out_shape=jax.ShapeDtypeStruct((lat // 8, 8, nj), BF),
            in_specs=[anyspace] * 6,
            out_specs=anyspace,
            scratch_shapes=[
                pltpu.VMEM((nt, nj, orders), BF),
                pltpu.VMEM((nt, rd), F32),
                pltpu.VMEM((1, n_deg, lat), BF),
                pltpu.VMEM((1, cols * rd, cols * rd), BF),
                pltpu.VMEM((n_deg,), jnp.int32),
                pltpu.VMEM((lat // 8, 8, nj), BF),
                pltpu.VMEM((lat // 8, 8, nj), BF),
                pltpu.VMEM((lat, nj), F32),
                pltpu.VMEM((n_deg, n_deg), BF),
                pltpu.VMEM((n_deg, lat), BF),
                pltpu.VMEM((lat, n_deg), BF),
                pltpu.VMEM((cols * rd, cols * rd), BF),
                pltpu.VMEM((na, nb, nj), BF),
                pltpu.VMEM((na, nb, nj), BF),
                pltpu.VMEM((pn.co, nb, pn.y, nj), BF),
                pltpu.VMEM(half, BF),
                pltpu.VMEM(half, BF),
                pltpu.VMEM((pn.co, nb, pn.y, nj), BF),
                pltpu.VMEM((na, nb, nj), BF),
                pltpu.VMEM((na, nb, nj), BF),
                pltpu.VMEM((lat // 8, 8, nj), BF),
                pltpu.SMEM((1,), jnp.int32),
                pltpu.SemaphoreType.DMA((6,)),
                pltpu.SemaphoreType.DMA((6, 2)),
                pltpu.SemaphoreType.DMA((6, 2)),
            ],
            compiler_params=pltpu.CompilerParams(
                collective_id=0, has_side_effects=True, vmem_limit_bytes=60 << 20),
        )(field, coef, table, inverses, degree_owner, order_ids)
        out = pl.pallas_call(
            unfold,
            grid=(1,),
            out_shape=jax.ShapeDtypeStruct((nt, nj, orders), BF),
            in_specs=[pl.BlockSpec((orders, nt // 8, 8, nj), lambda i: (0, 0, 0, 0))],
            out_specs=pl.BlockSpec((nt, nj, orders), lambda i: (0, 0, 0)),
            scratch_shapes=[pltpu.VMEM((orders * nt, nj), F32)],
        )(out.reshape(orders, nt // 8, 8, nj))
        out = out.reshape(nt, f, c, rd, orders)
        return jnp.transpose(out, (4, 0, 1, 2, 3))

    in_specs = (
        P(None, "row", None, None, "col"),
        P("row", "col"),
        P("row", None, None),
        P("row"),
        P(("row", "col"), None, None),
        P(),
    )
    return jax.shard_map(
        per_device, mesh=mesh, in_specs=in_specs,
        out_specs=P(None, "row", None, None, "col"), check_vma=False)
```
